256 devices in a mesh: ctx: 32 (over y, z), head: 8 (over x, core).
Axes of the slice: x: 4, y: 4, z: 8, core: 2. Of those that a mesh axis runs over, the one named last changes fastest.
Arguments:
- queries: bfloat16 [16384, 2048], P('ctx', 'head'), may hold values from -4.5 to 4.5
- keys: bfloat16 [16384, 1024], P('ctx', 'head'), may hold values from -4.5 to 4.5
- values: bfloat16 [16384, 1024], P('ctx', 'head'), may hold values from -4.5 to 4.5
- offsets: int32 [32], P('ctx'), may hold values from 0 to 512, as said below
- gate_logits: float32 [16], P('head'), may hold values from -2 to 2
- out_weight: bfloat16 [2048, 2048], P('head'), may hold values from -0.125 to 0.125
- grad_mixed: bfloat16 [16384, 2048], P('ctx', 'head'), may hold values from -6 to 6
Outputs:
- mixed: bfloat16 [16384, 2048], P('ctx', 'head')
- grad_queries: float32 [16384, 2048], P('ctx', 'head')
- grad_keys: float32 [16384, 1024], P('ctx', 'head')
- grad_values: float32 [16384, 1024], P('ctx', 'head')
- grad_weight: float32 [2048, 2048], P('head', 'ctx')
- grad_gates: float32 [16], P('head')
The draws below stay inside these ranges and needn't reach their ends.
Inputs may be any that keep to these rules, and one draw needn't show every extreme that they name: `offsets`: entry s is 512 where segment s continues the document of the segment before it, else the position within segment s at which a new document begins.
All inputs are finite; a program needn't handle non-finite values.
Results may differ from the reference program's by a relative error of at most 0.0064.
Values may be sent and summed in bfloat16 or wider, within the bound.
No kernel may reach another device: no remote copies, remote signals or barrier semaphores. Data moves between devices by JAX's collectives and lax.ppermute only.
A program may use at most 64 MiB of HBM per device.

```python
import jax
import jax.numpy as jnp
from jax import lax

D = 2048
HEADS = 16
KV_HEADS = 8
HEAD_DIM = 128
SEG = 512
TOKENS = 16384
NSEG = 32


def draw_pair(key):
    base = jax.random.fold_in(key, 7301)
    query_seed, key_seed = jax.random.split(base, 2)
    queries = jax.random.normal(query_seed, (TOKENS, HEADS * HEAD_DIM), jnp.float32)
    keys = jax.random.normal(key_seed, (TOKENS, KV_HEADS * HEAD_DIM), jnp.float32)
    queries = jnp.clip(queries, -4.5, 4.5)
    keys = jnp.clip(keys, -4.5, 4.5)
    return (queries, keys)


def draw_queries(key, part):
    return draw_pair(key)[0].astype(jnp.bfloat16)


def draw_keys(key, part):
    return draw_pair(key)[1].astype(jnp.bfloat16)


def draw_offsets(key, part):
    base = jax.random.fold_in(key, 9157)
    first_seed, second_seed, third_seed = jax.random.split(base, 3)
    resets = jax.random.randint(first_seed, (NSEG,), 0, 8)
    places = jax.random.randint(second_seed, (NSEG,), 0, SEG)
    half = NSEG // 2
    forced = jax.random.randint(third_seed, (), 0, half)
    index_row = jnp.arange(NSEG)
    chosen = jnp.where(resets == 0, places, SEG)
    chosen = jnp.where(index_row == forced, places, chosen)
    chosen = jnp.where(index_row == forced + half, SEG, chosen)
    return chosen.astype(jnp.int32)


def with_spikes(values, stream_key, source, target, shards_of, factor):
    def block_of(dim):
        return (jnp.arange(values.shape[dim]) // (values.shape[dim] // shards_of)).reshape((-1,) + (1,) * (values.ndim - 1 - dim))

    one_side = jax.random.permutation(stream_key, shards_of)[block_of(target)]
    second = (block_of(target) + shards_of // 2) % shards_of
    return jnp.where((block_of(source) == one_side) | (block_of(source) == second), factor * values, values)


def steps_of(own_key, dims, cuts, least, largest):
    factor_of, own = 1.0, jax.random.fold_in(own_key, 6)
    for dim, shards_of in cuts:
        heights = jnp.exp(jax.random.uniform(jax.random.fold_in(own, dim), (shards_of,), jnp.float32, least / len(cuts), largest / len(cuts)))
        factor_of = factor_of * jnp.repeat(heights, dims[dim] // shards_of).reshape([-1 if axis == dim else 1 for axis in range(len(dims))])
    return factor_of


def scatter_about(rng, shape, width, reach, cuts=(), dtype=jnp.bfloat16):
    values = jax.random.normal(rng, shape, jnp.float32) * width
    if len(cuts) > 0:
        values = steps_of(rng, shape, cuts, -0.22, 0.18) * values
    return jnp.clip(values, min=-reach, max=reach).astype(dtype)


def heavy_noise(key, extent, deviation, limit, cuts, heavy, dtype=jnp.bfloat16):
    result = deviation * jax.random.normal(key, extent, jnp.float32)
    if cuts:
        result = result * steps_of(key, extent, cuts, -0.22, 0.18)
    return jnp.clip(with_spikes(result, jax.random.fold_in(key, 3), *heavy), -limit, limit).astype(dtype)


def setup_inputs(seed: int = 0) -> dict:
    key_of = jax.random.split(jax.random.key(seed), 8)
    queries = draw_queries(jax.random.fold_in(key_of[7], 71), 0)
    keys = draw_keys(jax.random.fold_in(key_of[7], 71), 0)
    values = scatter_about(key_of[2], (TOKENS, KV_HEADS * HEAD_DIM), 1.0, 4.5, ((0, 32), (1, 8)))
    offsets = draw_offsets(jax.random.fold_in(key_of[7], 71), 0)
    gate_logits = jnp.clip(jax.random.uniform(key_of[4], (HEADS,), jnp.float32, -2.0, 2.0) * steps_of(key_of[4], (HEADS,), ((0, 8),), -0.4, 0.0), -2.0, 2.0)
    out_weight = scatter_about(key_of[5], (HEADS * HEAD_DIM, D), (HEADS * HEAD_DIM) ** -0.5, 0.125, ((0, 8),))
    grad_mixed = heavy_noise(key_of[6], (TOKENS, D), 1.0, 6.0, ((0, 32), (1, 8)), (0, 1, 32, 2.75))
    return {"queries": queries, "keys": keys, "values": values, "offsets": offsets, "gate_logits": gate_logits, "out_weight": out_weight, "grad_mixed": grad_mixed}


highest = lax.Precision.HIGHEST


def feature(inputs):
    return jnp.where(inputs > 0, inputs + 1.0, jnp.exp(jnp.minimum(inputs, 0.0)))


def feature_slope(inputs):
    return jnp.where(inputs > 0, 1.0, jnp.exp(jnp.minimum(inputs, 0.0)))


def reference(queries, keys, values, offsets, gate_logits, out_weight, grad_mixed):
    repeat = HEADS // KV_HEADS
    score_scale = HEAD_DIM ** -0.5
    query_blocks = queries.reshape(NSEG, SEG, KV_HEADS, repeat, HEAD_DIM)
    key_blocks = keys.reshape(NSEG, SEG, KV_HEADS, HEAD_DIM)
    value_blocks = values.reshape(NSEG, SEG, KV_HEADS, HEAD_DIM)
    position = jnp.arange(SEG).astype(jnp.int32)
    carry_factor = (offsets == SEG).astype(jnp.float32)
    sigmoid_gate = jax.nn.sigmoid(gate_logits.astype(jnp.float32)).reshape(KV_HEADS, repeat)
    mixing = sigmoid_gate[None, :, :, None]

    def deltas(element):
        key_seg, value_seg, offset = element
        counted = (position >= jnp.where(offset == SEG, 0, offset)).astype(jnp.float32)
        counted_feat = feature(key_seg.astype(jnp.float32)) * counted[:, None, None]
        memory = jnp.einsum("jgd,jge->gde", counted_feat, value_seg.astype(jnp.float32), precision=highest)
        return memory, jnp.sum(counted_feat, axis=0)

    delta_memory, delta_totals = lax.map(deltas, (key_blocks, value_blocks, offsets))

    def forward_step(running, element):
        memory, totals, factor = element
        return (factor * running[0] + memory, factor * running[1] + totals), running

    start = (jnp.zeros((KV_HEADS, HEAD_DIM, HEAD_DIM), jnp.float32), jnp.zeros((KV_HEADS, HEAD_DIM), jnp.float32))
    unused, (memory_in, totals_in) = lax.scan(forward_step, start, (delta_memory, delta_totals, carry_factor))
    grad_output = jnp.dot(grad_mixed, out_weight.T, preferred_element_type=jnp.float32).astype(jnp.bfloat16)
    grad_blocks = grad_output.reshape(NSEG, SEG, KV_HEADS, repeat, HEAD_DIM)

    def segment_pass(element):
        query_seg, key_seg, value_seg, offset, memory, totals, grad_seg = element
        query_float = query_seg.astype(jnp.float32)
        key_float = key_seg.astype(jnp.float32)
        value_float = value_seg.astype(jnp.float32)
        grad_float = grad_seg.astype(jnp.float32)
        retain = (position < offset).astype(jnp.float32)
        retained_feat = feature(query_float) * retain[:, None, None, None]
        numerator = jnp.einsum("igrd,gde->igre", retained_feat, memory, precision=highest)
        denominator = 1.0 + jnp.einsum("igrd,gd->igr", retained_feat, totals, precision=highest)
        recall = numerator / denominator[..., None]
        scores = jnp.einsum("igrd,jgd->grij", query_float, key_float, precision=highest) * score_scale
        later_doc = position >= offset
        allowed = (position[None, :] <= position[:, None]) & (later_doc[:, None] == later_doc[None, :])
        scores = jnp.where(allowed[None, None], scores, -1e30)
        scaled_exp = jnp.exp(scores - jnp.max(scores, axis=-1, keepdims=True))
        weights = scaled_exp / jnp.sum(scaled_exp, axis=-1, keepdims=True)
        weights_low = lax.optimization_barrier(weights.astype(jnp.bfloat16)).astype(jnp.float32)
        attend = jnp.einsum("grij,jgd->igrd", weights_low, value_float, precision=highest)
        output = (mixing * recall + (1.0 - mixing) * attend).astype(jnp.bfloat16)
        gate_terms = jnp.sum(grad_float * (recall - attend), axis=(0, 3))
        grad_recall = mixing * grad_float
        grad_attend = (1.0 - mixing) * grad_float
        grad_probs = jnp.einsum("igrd,jgd->grij", grad_attend, value_float, precision=highest)
        grad_scores = weights * (grad_probs - jnp.sum(grad_probs * weights, axis=-1, keepdims=True)) * score_scale
        grad_low = lax.optimization_barrier(grad_scores.astype(jnp.bfloat16)).astype(jnp.float32)
        grad_query = jnp.einsum("grij,jgd->igrd", grad_low, key_float, precision=highest)
        grad_key = jnp.einsum("grij,igrd->jgd", grad_low, query_float, precision=highest)
        grad_value = jnp.einsum("grij,igrd->jgd", weights_low, grad_attend, precision=highest)
        grad_numer = grad_recall / denominator[..., None]
        grad_denom = -jnp.sum(grad_recall * numerator, axis=-1) / (denominator * denominator)
        grad_feat = retain[:, None, None, None] * (jnp.einsum("igre,gde->igrd", grad_numer, memory, precision=highest) + grad_denom[..., None] * totals[None, :, None, :])
        grad_memory = jnp.einsum("igrd,igre->gde", retained_feat, grad_numer, precision=highest)
        grad_totals = jnp.einsum("igr,igrd->gd", grad_denom, retained_feat, precision=highest)
        grad_query = grad_query + grad_feat * feature_slope(query_float)
        return output, grad_query, grad_key, grad_value, grad_memory, grad_totals, gate_terms

    outputs = lax.map(segment_pass, (query_blocks, key_blocks, value_blocks, offsets, memory_in, totals_in, grad_blocks))
    output, grad_query, grad_key, grad_value, grad_memory, grad_totals, gate_terms = outputs

    def backward_step(running, element):
        memory, totals, factor = element
        return (memory + factor * running[0], totals + factor * running[1]), running

    unused_back, (flow_memory, flow_totals) = lax.scan(backward_step, start, (grad_memory, grad_totals, carry_factor), reverse=True)

    def key_pass(element):
        key_seg, value_seg, offset, memory, totals = element
        counted = (position >= jnp.where(offset == SEG, 0, offset)).astype(jnp.float32)[:, None, None]
        key_float = key_seg.astype(jnp.float32)
        value_float = value_seg.astype(jnp.float32)
        grad_key_feat = counted * (jnp.einsum("jge,gde->jgd", value_float, memory, precision=highest) + totals[None])
        grad_value_mem = counted * jnp.einsum("jgd,gde->jge", feature(key_float), memory, precision=highest)
        return grad_key_feat * feature_slope(key_float), grad_value_mem

    key_extra, value_extra = lax.map(key_pass, (key_blocks, value_blocks, offsets, flow_memory, flow_totals))
    out_flat = output.reshape(TOKENS, HEADS * HEAD_DIM)
    mixed = jnp.dot(out_flat, out_weight, preferred_element_type=jnp.float32).astype(jnp.bfloat16)
    grad_weight = jnp.dot(out_flat.T, grad_mixed, preferred_element_type=jnp.float32)
    grad_gates = (jnp.sum(gate_terms, axis=0) * sigmoid_gate * (1.0 - sigmoid_gate)).reshape(HEADS)
    grad_queries = grad_query.reshape(TOKENS, HEADS * HEAD_DIM)
    grad_keys = (grad_key + key_extra).reshape(TOKENS, KV_HEADS * HEAD_DIM)
    grad_values = (grad_value + value_extra).reshape(TOKENS, KV_HEADS * HEAD_DIM)
    return mixed, grad_queries, grad_keys, grad_values, grad_weight, grad_gates
```

```python
import functools

import jax
import jax.numpy as jnp
from jax import lax
from jax.experimental import pallas as pl
from jax.experimental.pallas import tpu as pltpu
from jax.sharding import Mesh
from jax.sharding import PartitionSpec as P

HD = 128
SEG = 512
BLK = 256
NY, NZ, NX, NC = 4, 8, 4, 2
PAY = 144
ROW = 136
SCALE = HD ** (-0.5)
f32 = jnp.float32
bf16 = jnp.bfloat16
highest = lax.Precision.HIGHEST


VM = pl.BlockSpec(memory_space=pltpu.VMEM)
SM = pl.BlockSpec(memory_space=pltpu.SMEM)


def call(kernel, out_shape, in_specs, out_specs, name, flops, nbytes):
    return pl.pallas_call(
        kernel,
        out_shape=out_shape,
        in_specs=in_specs,
        out_specs=out_specs,
        name=name,
        compiler_params=pltpu.CompilerParams(vmem_limit_bytes=40 << 20),
        cost_estimate=pl.CostEstimate(flops=flops, bytes_accessed=nbytes, transcendentals=0),
    )


def sds(shape, dtype):
    return jax.ShapeDtypeStruct(shape, dtype)


def dot(a, b, dims, precision=None):
    return lax.dot_general(a, b, (dims, ((), ())), precision=precision, preferred_element_type=f32)


NN = ((1,), (0,))
NT = ((1,), (1,))
TN = ((0,), (0,))


def feature(x):
    return jnp.where(x > 0, x + 1.0, jnp.exp(jnp.minimum(x, 0.0)))


def slope(x):
    return jnp.where(x > 0, 1.0, jnp.exp(jnp.minimum(x, 0.0)))


def rows_of(shape):
    return lax.broadcasted_iota(jnp.int32, shape, 0)


def sigmoid_row(logit):
    return 1.0 / (1.0 + jnp.exp(-jnp.full((1, HD), logit, f32)))


def parts_of(x):
    hi = x.astype(bf16).astype(f32)
    mid = (x - hi).astype(bf16).astype(f32)
    return hi, mid, x - hi - mid


def stacked(rows, height):
    index = rows_of((height, HD))
    out = jnp.zeros((height, HD), f32)
    for k, row in enumerate(rows):
        out = jnp.where(index == k, jnp.broadcast_to(row, (height, HD)), out)
    return out


def counted_mask(o):
    start = jnp.where(o == SEG, 0, o)
    return (rows_of((SEG, HD)) >= start).astype(f32)


def carry_row(o):
    return jnp.full((1, HD), jnp.where(o == SEG, 1.0, 0.0).astype(f32), f32)


def delta_kernel(o_ref, k_ref, v_ref, pay_ref):
    o = o_ref[0]
    feat = feature(k_ref[...].astype(f32)) * counted_mask(o)
    memory = dot(feat, v_ref[...].astype(f32), TN, highest)
    totals = jnp.sum(feat, axis=0, keepdims=True)
    tail = stacked((*parts_of(totals), carry_row(o)), PAY - HD)
    low, tail = memory.astype(bf16), tail.astype(bf16)
    for k in range(NZ):
        pay_ref[k, :HD, :] = low
        pay_ref[k, HD:, :] = tail


def row_kernel(backward, pay_ref, inside_ref, total_ref):
    z = lax.axis_index("z")
    run_m = jnp.zeros((HD, HD), f32)
    run_t = jnp.zeros((1, HD), f32)
    run_c = jnp.ones((1, HD), f32)
    in_m, in_t, in_c = run_m, run_t, run_c
    gates = [jnp.zeros((1, HD), f32), jnp.zeros((1, HD), f32)]
    for k in reversed(range(NZ)) if backward else range(NZ):
        memory = pay_ref[k, :HD, :].astype(f32)
        tail = pay_ref[k, HD:, :].astype(f32)
        totals = tail[0:1] + tail[1:2] + tail[2:3]
        c = tail[3:4]
        run_m, run_t, run_c = c * run_m + memory, c * run_t + totals, c * run_c
        take = (k > z) if backward else (k < z)
        in_m = jnp.where(take, run_m, in_m)
        in_t = jnp.where(take, run_t, in_t)
        in_c = jnp.where(take, run_c, in_c)
        if backward:
            for h in range(2):
                at = 4 + 3 * h
                gates[h] = gates[h] + (tail[at : at + 1] + tail[at + 1 : at + 2] + tail[at + 2 : at + 3])
    inside_ref[:HD, :] = in_m
    inside_ref[HD:, :] = stacked((in_t, in_c, *gates), ROW - HD)
    total_ref[:HD, :] = run_m
    total_ref[HD:, :] = stacked((run_t, run_c, *gates), ROW - HD)


def joined(inside_ref, refs, keep):
    run_m = jnp.zeros((HD, HD), f32)
    run_t = jnp.zeros((1, HD), f32)
    for ref, kept in zip(refs, keep):
        c = ref[HD + 1 : HD + 2, :]
        new_m = c * run_m + ref[:HD, :]
        new_t = c * run_t + ref[HD : HD + 1, :]
        run_m = jnp.where(kept, new_m, run_m)
        run_t = jnp.where(kept, new_t, run_t)
    c = inside_ref[HD + 1 : HD + 2, :]
    return inside_ref[:HD, :] + c * run_m, inside_ref[HD : HD + 1, :] + c * run_t


def block_of(k, other):
    x, c = lax.axis_index("x"), lax.axis_index("c")
    chip = lax.rem(x + (NX - k), NX)
    return chip, (1 - c) if other else c


def local_kernel(o_ref, gate_ref, q_ref, k_ref, v_ref, w_ref, *rest):
    cots, (attend_ref, ga_ref, ql_ref, kl_ref, vl_ref) = rest[:8], rest[8:]
    o = o_ref[0]
    acc = jnp.zeros((SEG, BLK), f32)
    for n, cot_ref in enumerate(cots):
        chip, core = block_of(n % NX, n >= NX)
        at = pl.multiple_of((chip * NC + core) * BLK, BLK)
        acc = acc + dot(cot_ref[...], w_ref[:, pl.ds(at, BLK)], NT)
    ga = acc.astype(bf16)
    ga_ref[...] = ga
    T = 128
    k_all, v_all = k_ref[...], v_ref[...]
    kl = [jnp.zeros((T, HD), f32) for _ in range(SEG // T)]
    vl = [jnp.zeros((T, HD), f32) for _ in range(SEG // T)]
    for h in range(2):
        complement = 1.0 - sigmoid_row(gate_ref[h])
        comp = complement[0:1, 0:1]
        for i in range(SEG // T):
            n = (i + 1) * T
            rows, cols = slice(i * T, n), slice(0, n)
            lanes = slice(h * HD, (h + 1) * HD)
            q = q_ref[rows, lanes]
            g = ga[rows, lanes]
            k, v = k_all[cols], v_all[cols]
            pi = lax.broadcasted_iota(jnp.int32, (T, n), 0) + i * T
            pj = lax.broadcasted_iota(jnp.int32, (T, n), 1)
            allowed = (pj <= pi) & ((pj >= o) | (pi < o))
            s = jnp.where(allowed, dot(q, k, NT) * SCALE, -1e30)
            e = jnp.exp(s - jnp.max(s, axis=1, keepdims=True))
            w = e * (1.0 / jnp.sum(e, axis=1, keepdims=True))
            low = w.astype(bf16)
            attend_ref[rows, lanes] = dot(low, v, NN)
            gp = comp * dot(g, v, NT)
            gs = w * (gp - jnp.sum(gp * w, axis=1, keepdims=True)) * SCALE
            gl = gs.astype(bf16)
            ql_ref[rows, lanes] = dot(gl, k, NN)
            dk = dot(gl, q, TN)
            dv = dot(low, g, TN) * complement
            for b in range(i + 1):
                kl[b] = kl[b] + dk[b * T : (b + 1) * T]
                vl[b] = vl[b] + dv[b * T : (b + 1) * T]
    for b in range(SEG // T):
        kl_ref[b * T : (b + 1) * T, :] = kl[b]
        vl_ref[b * T : (b + 1) * T, :] = vl[b]


def retained_mask(o):
    return (rows_of((SEG, HD)) < o).astype(f32)


def recall_of(q, o, memory, totals):
    feat = feature(q) * retained_mask(o)
    numer = dot(feat, memory, NN, highest)
    denom = 1.0 + jnp.sum(feat * totals, axis=1, keepdims=True)
    return feat, numer, denom


def attention_kernel(o_ref, gate_ref, inside_ref, r3_ref, r2_ref, r1_ref, q_ref, attend_ref, *rest):
    cots, (att_ref, state_ref, pay_ref) = rest[:8], rest[8:]
    o = o_ref[0]
    memory, totals = joined(inside_ref, (r3_ref, r2_ref, r1_ref), (True, True, True))
    state_ref[:HD, :] = memory
    state_ref[HD:, :] = jnp.broadcast_to(totals, (ROW - HD, HD))
    for h in range(2):
        lanes = slice(h * HD, (h + 1) * HD)
        gate = sigmoid_row(gate_ref[h])
        feat, numer, denom = recall_of(q_ref[:, lanes].astype(f32), o, memory, totals)
        recall = numer / denom
        att_ref[:, lanes] = (gate * recall + (1.0 - gate) * attend_ref[:, lanes]).astype(bf16)
    att = att_ref[...]
    for n, cot_ref in enumerate(cots):
        chip, core = block_of(n % NX, n >= NX)
        at = pl.multiple_of(core * BLK, BLK)
        pay_ref[chip, :, pl.ds(at, BLK)] = dot(att, cot_ref[...], TN).astype(bf16)


def grad_kernel(o_ref, gate_ref, state_ref, q_ref, attend_ref, ga_ref, pay_ref):
    o = o_ref[0]
    memory, totals = state_ref[:HD, :], state_ref[HD : HD + 1, :]
    gm = jnp.zeros((HD, HD), f32)
    gt = jnp.zeros((1, HD), f32)
    rows = []
    for h in range(2):
        lanes = slice(h * HD, (h + 1) * HD)
        gate = sigmoid_row(gate_ref[h])
        feat, numer, denom = recall_of(q_ref[:, lanes].astype(f32), o, memory, totals)
        ga = ga_ref[:, lanes].astype(f32)
        inv = 1.0 / denom
        gr = gate * ga
        gn = gr * inv
        gd = -jnp.sum(gr * numer, axis=1, keepdims=True) * (inv * inv)
        gm = gm + dot(feat, gn, TN, highest)
        gt = gt + jnp.sum(feat * gd, axis=0, keepdims=True)
        terms = jnp.sum(ga * (numer * inv - attend_ref[:, lanes]), axis=0, keepdims=True)
        total = jnp.sum(terms, axis=1, keepdims=True) * gate * (1.0 - gate)
        rows.extend(parts_of(total))
    tail = stacked((*parts_of(gt), carry_row(o), *rows), PAY - HD).astype(bf16)
    low = gm.astype(bf16)
    for k in range(NZ):
        pay_ref[k, :HD, :] = low
        pay_ref[k, HD:, :] = tail


def queries_kernel(o_ref, gate_ref, state_ref, q_ref, ga_ref, ql_ref, gq_ref):
    o = o_ref[0]
    memory, totals = state_ref[:HD, :], state_ref[HD : HD + 1, :]
    for h in range(2):
        lanes = slice(h * HD, (h + 1) * HD)
        gate = sigmoid_row(gate_ref[h])
        q = q_ref[:, lanes].astype(f32)
        feat, numer, denom = recall_of(q, o, memory, totals)
        inv = 1.0 / denom
        gr = gate * ga_ref[:, lanes].astype(f32)
        gd = -jnp.sum(gr * numer, axis=1, keepdims=True) * (inv * inv)
        gf = retained_mask(o) * (dot(gr * inv, memory, NT, highest) + gd * totals)
        gq_ref[:, lanes] = ql_ref[:, lanes] + gf * slope(q)


def mixed_kernel(att_ref, other_ref, w_ref, wo_ref, *outs):
    x, c = lax.axis_index("x"), lax.axis_index("c")
    for k, out_ref in enumerate(outs):
        chip = lax.rem(x + k, NX)
        at = pl.multiple_of((chip * NC + c) * BLK, BLK)
        here = dot(att_ref[...], w_ref[:, pl.ds(at, BLK)], NN)
        there = dot(other_ref[...], wo_ref[:, pl.ds(pl.multiple_of(chip * BLK, BLK), BLK)], NN)
        out_ref[...] = (here + there).astype(out_ref.dtype)


def halves_kernel(w_ref, out_ref):
    c = lax.axis_index("c")
    for chip in range(NX):
        at = pl.multiple_of((chip * NC + 1 - c) * BLK, BLK)
        out_ref[:, chip * BLK : (chip + 1) * BLK] = w_ref[:, pl.ds(at, BLK)]


def mixed_sum_kernel(s_ref, a_ref, b_ref, c_ref, out_ref):
    total = s_ref[...] + a_ref[...].astype(f32) + b_ref[...].astype(f32) + c_ref[...].astype(f32)
    out_ref[...] = total.astype(bf16)


def weight_mid_kernel(in_ref, out_ref):
    total = in_ref[0].astype(f32)
    for k in range(1, NY):
        total = total + in_ref[k].astype(f32)
    turned = total.T.astype(bf16)
    for k in range(NZ):
        out_ref[k] = turned[k * 64 : (k + 1) * 64]


def weight_end_kernel(in_ref, out_ref):
    total = in_ref[0].astype(f32)
    for k in range(1, NZ):
        total = total + in_ref[k].astype(f32)
    out_ref[...] = total.T


def final_kernel(o_ref, inside_ref, total_ref, r3_ref, r2_ref, r1_ref, k_ref, v_ref, kl_ref, vl_ref, gk_ref, gv_ref, gg_ref):
    o = o_ref[0]
    y = lax.axis_index("y")
    keep = (y + 3 < NY, y + 2 < NY, y + 1 < NY)
    flow, flow_totals = joined(inside_ref, (r3_ref, r2_ref, r1_ref), keep)
    counted = counted_mask(o)
    k = k_ref[...].astype(f32)
    gk = dot(v_ref[...].astype(f32), flow, NT, highest) + flow_totals
    gk_ref[...] = kl_ref[...] + counted * gk * slope(k)
    gv_ref[...] = vl_ref[...] + dot(counted * feature(k), flow, NN, highest)
    for h in range(2):
        at = HD + 2 + h
        total = total_ref[at : at + 1, 0:1]
        for ref in (r3_ref, r2_ref, r1_ref):
            total = total + ref[at : at + 1, 0:1]
        gg_ref[h] = total[0, 0]


def shift(v, axis, k, size, wrap=True):
    pairs = [(i, (i + k) % size) for i in range(size) if wrap or 0 <= i + k < size]
    return lax.ppermute(v, axis, pairs)


def exchange(v, axis):
    return lax.all_to_all(v, axis, split_axis=0, concat_axis=0, tiled=True)


def body(queries, keys, values, offsets, gate_logits, out_weight, grad_mixed):
    cots = [grad_mixed] + [shift(grad_mixed, "x", k, NX) for k in range(1, NX)]
    cots = cots + [shift(v, "c", 1, NC) for v in cots]
    halves = call(halves_kernel, sds((BLK, NX * BLK), bf16), [VM], VM, "halves", 0, 1 << 20)(out_weight)
    other_weight = shift(halves, "c", 1, NC)

    pay = call(delta_kernel, sds((NZ, PAY, HD), bf16), [SM, VM, VM], VM, "delta", 1 << 26, 1 << 19)(offsets, keys, values)
    pay = exchange(pay, "z")
    state = sds((ROW, HD), f32)
    inside, total = call(functools.partial(row_kernel, False), (state, state), [VM], (VM, VM), "row_fwd", 1 << 20, 1 << 19)(pay)
    earlier = [shift(total, "y", k, NY, False) for k in (3, 2, 1)]

    wide = sds((SEG, BLK), f32)
    narrow = sds((SEG, HD), f32)
    attend, ga, ql, kl, vl = call(
        local_kernel, (wide, sds((SEG, BLK), bf16), wide, narrow, narrow), [SM, SM] + [VM] * 12, (VM,) * 5, "local", 1 << 31, 6 << 20
    )(offsets, gate_logits, queries, keys, values, out_weight, *cots)

    att, memory, terms = call(
        attention_kernel,
        (sds((SEG, BLK), bf16), state, sds((NY, BLK, 2 * BLK), bf16)),
        [SM, SM] + [VM] * 14,
        (VM,) * 3,
        "attention",
        1 << 29,
        5 << 20,
    )(offsets, gate_logits, inside, *earlier, queries, attend, *cots)
    terms = exchange(terms, "y")
    other_att = shift(att, "c", 1, NC)

    pay = call(grad_kernel, sds((NZ, PAY, HD), bf16), [SM, SM] + [VM] * 4, VM, "grad", 1 << 27, 2 << 20)(
        offsets, gate_logits, memory, queries, attend, ga
    )
    pay = exchange(pay, "z")

    low = sds((SEG, BLK), bf16)
    sums = call(mixed_kernel, (wide, low, low, low), [VM] * 4, (VM,) * 4, "mixed", 1 << 29, 3 << 20)(
        att, other_att, out_weight, other_weight
    )
    others = [shift(sums[k], "x", k, NX) for k in range(1, NX)]

    gq = call(queries_kernel, wide, [SM, SM] + [VM] * 4, VM, "queries", 1 << 27, 2 << 20)(
        offsets, gate_logits, memory, queries, ga, ql
    )

    terms = call(weight_mid_kernel, sds((NZ, 64, BLK), bf16), [VM], VM, "weight_mid", 1 << 20, 1 << 20)(terms)
    terms = exchange(terms, "z")

    inside, total = call(functools.partial(row_kernel, True), (state, state), [VM], (VM, VM), "row_bwd", 1 << 20, 1 << 19)(pay)
    later = [shift(total, "y", -k, NY) for k in (3, 2, 1)]
    gk, gv, gg = call(
        final_kernel, (narrow, narrow, sds((2,), f32)), [SM] + [VM] * 9, (VM, VM, SM), "final", 1 << 26, 2 << 20
    )(offsets, inside, total, *later, keys, values, kl, vl)

    mixed = call(mixed_sum_kernel, low, [VM] * 4, VM, "mixed_sum", 1 << 20, 1 << 20)(sums[0], *others)
    gw = call(weight_end_kernel, sds((BLK, 64), f32), [VM], VM, "weight_end", 1 << 20, 1 << 19)(terms)
    return mixed, gq, gk, gv, gw, gg


def solution(mesh):
    torus = Mesh(mesh.devices.reshape(NY, NZ, NX, NC), ("y", "z", "x", "c"))
    ctx, head = ("y", "z"), ("x", "c")
    in_specs = (P(ctx, head), P(ctx, head), P(ctx, head), P(ctx), P(head), P(head, None), P(ctx, head))
    out_specs = (P(ctx, head), P(ctx, head), P(ctx, head), P(ctx, head), P(head, ctx), P(head))
    return jax.shard_map(body, mesh=torus, in_specs=in_specs, out_specs=out_specs, check_vma=False)
```
